32 devices in a mesh: rcp: 4 (over y, x), lon: 8 (over z, core).
Axes of the slice: x: 2, y: 2, z: 4, core: 2. Of those that a mesh axis runs over, the one named last changes fastest.
Arguments:
- adj_in: float32 [32, 32, 128, 128], P('rcp', None, 'lon'), may hold values from -6 to 6
- mass_flux: float32 [4, 2, 6, 32, 128, 128], P('rcp', None, None, None, 'lon'), may hold values from -0.24 to 0.24
- mixing: float32 [4, 128, 32, 32], P('rcp', 'lon'), may hold values from 0 to 0.7, as said below
- window_owner: int32 [6], replicated, may hold values from 0 to 3
- receptor_lon: int32 [32], P('rcp'), may hold values from 0 to 127
- receptor_lat: int32 [32], P('rcp'), may hold values from 0 to 127
- release_step: int32 [32], P('rcp'), may hold values from 0 to 5
Outputs:
- adj_out: float32 [32, 32, 128, 128], P('rcp', None, 'lon')
- footprint: float32 [32, 128, 128], P('rcp', 'lon')
The draws below stay inside these ranges and needn't reach their ends.
Inputs may be any that keep to these rules, and one draw needn't show every extreme that they name: `mixing`: every entry is non-negative.
All inputs are finite; a program needn't handle non-finite values.
Results may differ from the reference program's by a relative error of at most 0.0003.
Values sent between devices are 32-bit elements; how exact they have to be, the bound alone decides.
No kernel may reach another device: no remote copies, remote signals or barrier semaphores. Data moves between devices by JAX's collectives and lax.ppermute only.
A program may use at most 128 MiB of HBM per device.

```python
import jax
import jax.numpy as jnp
from jax import lax

LAT = 128
LEV = 32
STEPS = 6
NLON = 128
RECEPTORS = 32
N_RCP = 4


def draw_mixing(key, part):
    first, second = jax.random.split(key)
    shape = (N_RCP, NLON, LEV, LEV)
    off_diag = jax.random.uniform(first, shape, jnp.float32, 0.0, 0.8 / LEV)
    diag = jax.random.uniform(second, (N_RCP, NLON, LEV), jnp.float32, 0.4, 0.7)
    identity = jnp.eye(LEV, dtype=jnp.float32)
    return off_diag * (1.0 - identity) + diag[..., None] * identity


def with_ends(values, rng, smallest, top_value):
    index_at = [jax.random.randint(jax.random.fold_in(rng, axis), (), 0, length) for axis, length in enumerate(values.shape)]
    longest = values.shape.index(max(values.shape))
    next_to = index_at[:longest] + [(index_at[longest] + 1) % values.shape[longest]] + index_at[longest + 1:]
    return values.at[tuple(index_at)].set(smallest).at[tuple(next_to)].set(top_value)


def shard_levels(stream_key, dims, pieces, low, largest):
    def one(dim, parts):
        draws = jax.random.uniform(jax.random.fold_in(jax.random.fold_in(stream_key, 6), dim), (parts,), jnp.float32, low / len(pieces), largest / len(pieces))
        return jnp.repeat(jnp.exp(draws), dims[dim] // parts).reshape((-1,) + (1,) * (len(dims) - dim - 1))

    level = one(*pieces[0])
    for cut in pieces[1:]:
        level = level * one(*cut)
    return level


def scatter_about(key, shape, width, most, cuts=(), kind=jnp.bfloat16):
    result = jax.random.normal(key, shape, jnp.float32) * width
    if len(cuts) > 0:
        result = shard_levels(key, shape, cuts, -0.22, 0.18) * result
    return jnp.clip(result, min=-most, max=most).astype(kind)


def setup_inputs(seed: int = 0) -> dict:
    key_list = jax.random.split(jax.random.key(seed), 8)
    adj_in = scatter_about(key_list[0], (RECEPTORS, LEV, NLON, LAT), 1.0, 6.0, ((0, 4), (2, 8)), jnp.float32)
    mass_flux = jnp.clip(jax.random.uniform(key_list[1], (N_RCP, 2, STEPS, LEV, NLON, LAT), jnp.float32, -0.24, 0.24) * shard_levels(key_list[1], (N_RCP, 2, STEPS, LEV, NLON, LAT), ((0, 4), (4, 8)), -0.4, 0.0), -0.24, 0.24)
    mixing = draw_mixing(jax.random.fold_in(key_list[7], 71), 0)
    window_owner = with_ends(jax.random.randint(key_list[3], (STEPS,), 0, N_RCP), jax.random.fold_in(key_list[3], 1), 0, N_RCP - 1).astype(jnp.int32)
    receptor_lon = with_ends(jax.random.randint(key_list[4], (RECEPTORS,), 0, NLON), jax.random.fold_in(key_list[4], 1), 0, NLON - 1).astype(jnp.int32)
    receptor_lat = with_ends(jax.random.randint(key_list[5], (RECEPTORS,), 0, LAT), jax.random.fold_in(key_list[5], 1), 0, LAT - 1).astype(jnp.int32)
    release_step = with_ends(jax.random.randint(key_list[6], (RECEPTORS,), 0, STEPS), jax.random.fold_in(key_list[6], 1), 0, STEPS - 1).astype(jnp.int32)
    return dict(adj_in=adj_in, mass_flux=mass_flux, mixing=mixing, window_owner=window_owner, receptor_lon=receptor_lon, receptor_lat=receptor_lat, release_step=release_step)


def one_receptor(flux_u, flux_v, mats, item):
    field, rlon, rlat, rel = item
    lons = jnp.arange(NLON, dtype=jnp.int32)
    lats = jnp.arange(LAT, dtype=jnp.int32)
    lat_index = lax.broadcasted_iota(jnp.int32, flux_v.shape, 3)
    v_south = jnp.where(lat_index > 0, flux_v, jnp.float32(0.0))
    zero_row = jnp.zeros((LEV, NLON, 1), jnp.float32)
    foot = jnp.zeros((NLON, LAT), jnp.float32)
    for s in range(STEPS):
        hit = ((lons[:, None] == rlon) & (lats[None, :] == rlat) & (rel == s)).astype(jnp.float32)
        field = field.at[0].add(hit)
        u_west = flux_u[s]
        u_east = jnp.roll(u_west, -1, axis=1)
        left = jnp.roll(field, 1, axis=1)
        right = jnp.roll(field, -1, axis=1)
        west = jnp.maximum(u_west, 0.0) * left + jnp.minimum(u_west, 0.0) * field
        east = jnp.maximum(u_east, 0.0) * field + jnp.minimum(u_east, 0.0) * right
        vs = v_south[s]
        vn = jnp.concatenate([vs[:, :, 1:], zero_row], axis=2)
        below = jnp.concatenate([zero_row, field[:, :, :-1]], axis=2)
        above = jnp.concatenate([field[:, :, 1:], zero_row], axis=2)
        south = jnp.maximum(vs, 0.0) * below + jnp.minimum(vs, 0.0) * field
        north = jnp.maximum(vn, 0.0) * field + jnp.minimum(vn, 0.0) * above
        moved = field + west - east + south - north
        field = jnp.einsum("kab,bky->aky", mats[s], moved, precision=lax.Precision.HIGHEST, preferred_element_type=jnp.float32)
        foot = foot + field[0]
    return field, foot


def reference(adj_in, mass_flux, mixing, window_owner, receptor_lon, receptor_lat, release_step):
    flux_steps = []
    mat_steps = []
    for s in range(STEPS):
        owner = window_owner[s]
        slot = lax.dynamic_index_in_dim(mass_flux, owner, 0, keepdims=False)
        flux_steps.append(slot[:, s])
        mat_steps.append(lax.dynamic_index_in_dim(mixing, owner, 0, keepdims=False))
    flux = jnp.stack(flux_steps, axis=1)
    mats = jnp.stack(mat_steps, axis=0)
    work = lambda item: one_receptor(flux[0], flux[1], mats, item)
    adj_out, footprint = lax.map(work, (adj_in, receptor_lon, receptor_lat, release_step))
    return adj_out, footprint
```

```python
import functools

import jax
import jax.numpy as jnp
from jax import lax
from jax.experimental import pallas as pl
from jax.experimental.pallas import tpu as pltpu
from jax.sharding import PartitionSpec as P

CHUNKS = ((0, 1, 2), (3, 4), (5,))


def flip(block, bit):
    count = lax.axis_size("rcp")
    return lax.ppermute(block, "rcp", [(i, i ^ (1 << bit)) for i in range(count)])


def along(block, distance):
    count = lax.axis_size("lon")
    return lax.ppermute(block, "lon", [(i, (i + distance) % count) for i in range(count)])


def from_owner(block, owners, order):
    count = lax.axis_size("rcp")
    if count & (count - 1) or block.shape[1] % count:
        mine = owners == lax.axis_index("rcp")
        return lax.psum(jnp.where(mine[:, None, None, None], block, 0.0), "rcp")
    me = lax.axis_index("rcp")
    for bit in order:
        side = (me >> bit) & 1
        half = block.shape[1] // 2
        send = lax.dynamic_slice_in_dim(block, (1 - side) * half, half, axis=1)
        keep = lax.dynamic_slice_in_dim(block, side * half, half, axis=1)
        got = flip(send, bit)
        same = ((owners >> bit) & 1) == side
        block = jnp.where(same[:, None, None, None], keep, got)
    for bit in order[::-1]:
        side = (me >> bit) & 1
        got = flip(block, bit)
        block = jnp.where(
            side == 0,
            jnp.concatenate([block, got], axis=1),
            jnp.concatenate([got, block], axis=1),
        )
    return block


def gather_slots(block):
    count = lax.axis_size("rcp")
    if count & (count - 1):
        return lax.all_gather(block, "rcp", axis=0, tiled=True)
    me = lax.axis_index("rcp")
    for bit in range(count.bit_length() - 1):
        side = (me >> bit) & 1
        got = flip(block, bit)
        block = jnp.where(
            side == 0,
            jnp.concatenate([block, got], axis=0),
            jnp.concatenate([got, block], axis=0),
        )
    return block


def steps_kernel(steps, total, reach, owner_ref, rlon_ref, rlat_ref, rel_ref, start_ref,
                 field_hbm, foot_ref, u_ref, v_ref, mats_ref, out_ref, foot_out_ref,
                 field_ref, other_ref, sem):
    count, ext, lev, lat = field_ref.shape
    halo = total
    width = ext - 2 * halo
    nlon = width * lax.axis_size("lon")
    load = pltpu.make_async_copy(field_hbm, field_ref, sem)
    load.start()
    foot_out_ref[...] = foot_ref[...]
    lane = lax.broadcasted_iota(jnp.int32, (lev, lat), 1)
    lane_row = lax.broadcasted_iota(jnp.int32, (1, lat), 1)
    first = lane == 0
    last = lane == lat - 1

    load.wait()
    bufs = [(field_ref, other_ref)[k % 2] for k in range(len(steps))] + [out_ref]
    for k, step in enumerate(steps):
        src, dst = bufs[k], bufs[k + 1]
        owner = owner_ref[step]
        for r in range(count):
            col = lax.rem(rlon_ref[r] - start_ref[0] + halo + nlon, nlon)

            @pl.when((rel_ref[r] == step) & (col < ext))
            def _():
                row = src[r, pl.ds(col, 1), 0:1, :]
                src[r, pl.ds(col, 1), 0:1, :] = row + jnp.where(
                    lane_row == rlat_ref[r], 1.0, 0.0
                )[None]

        def column(c, carry, src=src, dst=dst, k=k, owner=owner):
            j = c - halo + reach
            uw = u_ref[k, j]
            ue = u_ref[k, j + 1]
            vs = jnp.where(first, 0.0, v_ref[k, j])
            vn = jnp.where(last, 0.0, pltpu.roll(v_ref[k, j], lat - 1, 1))
            cw = jnp.maximum(uw, 0.0)
            ce = -jnp.minimum(ue, 0.0)
            cs = jnp.maximum(vs, 0.0)
            cn = -jnp.minimum(vn, 0.0)
            c0 = 1.0 + (jnp.minimum(uw, 0.0) - jnp.maximum(ue, 0.0)) + (
                jnp.minimum(vs, 0.0) - jnp.maximum(vn, 0.0)
            )
            his, los = [], []
            for r in range(count):
                q = src[r, c]
                p = c0 * q + cw * src[r, c - 1] + ce * src[r, c + 1]
                p = p + cs * pltpu.roll(q, 1, 1) + cn * pltpu.roll(q, lat - 1, 1)
                hi = p.astype(jnp.bfloat16)
                his.append(hi)
                los.append((p - hi.astype(jnp.float32)).astype(jnp.bfloat16))
            hi = jnp.concatenate(his, axis=1)
            lo = jnp.concatenate(los, axis=1)
            new = jnp.dot(
                mats_ref[owner * ext + c],
                jnp.concatenate([hi, lo, hi], axis=0),
                preferred_element_type=jnp.float32,
            )
            for r in range(count):
                dst[r, c] = new[:, r * lat:(r + 1) * lat]

            @pl.when((c >= halo) & (c < halo + width))
            def _():
                for r in range(count):
                    row = foot_out_ref[r, pl.ds(c - halo, 1), :]
                    foot_out_ref[r, pl.ds(c - halo, 1), :] = row + new[0:1, r * lat:(r + 1) * lat]

            return carry

        lax.fori_loop(step + 1, ext - step - 1, column, 0)


def run_steps(steps, total, reach, scalars, field, foot, u, v, mats):
    smem = pl.BlockSpec(memory_space=pltpu.SMEM)
    vmem = pl.BlockSpec(memory_space=pltpu.VMEM)
    return pl.pallas_call(
        functools.partial(steps_kernel, steps, total, reach),
        out_shape=(
            jax.ShapeDtypeStruct(field.shape, jnp.float32),
            jax.ShapeDtypeStruct(foot.shape, jnp.float32),
        ),
        in_specs=[smem] * 5 + [pl.BlockSpec(memory_space=pl.ANY)] + [vmem] * 4,
        out_specs=(vmem, vmem),
        scratch_shapes=[pltpu.VMEM(field.shape, jnp.float32)] * 2 + [pltpu.SemaphoreType.DMA],
        compiler_params=pltpu.CompilerParams(vmem_limit_bytes=48 << 20),
        cost_estimate=pl.CostEstimate(
            flops=int(len(steps) * field.size * 200), bytes_accessed=int(field.size * 8),
            transcendentals=0,
        ),
        name="steps_%d" % steps[0],
    )(*scalars, field, foot, u, v, mats)


def local(adj_in, mass_flux, mixing, window_owner, receptor_lon, receptor_lat, release_step):
    count, lev, width, lat = adj_in.shape
    total = mass_flux.shape[2]
    start = (lax.axis_index("lon") * width).astype(jnp.int32)[None]
    scalars = (window_owner, receptor_lon, receptor_lat, release_step, start)
    bits = tuple(range((lax.axis_size("rcp") - 1).bit_length()))

    field = adj_in.transpose(0, 2, 1, 3)
    west = along(field[:, width - total:], 1)
    east = along(field[:, :total], -1)
    field = jnp.concatenate([west, field, east], axis=1)
    ext = width + 2 * total

    mats = mixing[0]
    mats_west = along(mats[width - total:], 1)
    mats_east = along(mats[:total], -1)
    mats = jnp.concatenate([mats_west, mats, mats_east], axis=0)
    pack = lat // lev
    mats = mats.reshape(ext // pack, pack, lev, lev).transpose(0, 2, 1, 3)
    mats = gather_slots(mats.reshape(1, ext // pack, lev, pack * lev))
    slots = mats.shape[0]
    mats = mats.reshape(slots, ext // pack, lev, pack, lev).transpose(0, 1, 3, 2, 4)
    mats = mats.reshape(slots * ext, lev, lev)
    high = lax.reduce_precision(mats, exponent_bits=8, mantissa_bits=7)
    mats = jnp.concatenate([high, high, mats - high], axis=2).astype(jnp.bfloat16)

    flux = mass_flux[0].transpose(0, 1, 3, 2, 4)
    foot = jnp.zeros((count, width, lat), jnp.float32)
    for steps in CHUNKS:
        reach = total - 1 - steps[0]
        owners = jnp.stack([window_owner[s] for s in steps])
        rows = slice(steps[0], steps[-1] + 1)
        u = from_owner(flux[0, rows], owners, bits)
        v = from_owner(flux[1, rows], owners, bits[::-1])
        right = along(u[:, :reach + 1] if reach == 0 else jnp.concatenate([u[:, :reach + 1], v[:, :reach]], axis=1), -1)
        if reach:
            left = along(jnp.concatenate([u[:, width - reach:], v[:, width - reach:]], axis=1), 1)
            u = jnp.concatenate([left[:, :reach], u, right[:, :reach + 1]], axis=1)
            v = jnp.concatenate([left[:, reach:], v, right[:, reach + 1:]], axis=1)
        else:
            u = jnp.concatenate([u, right], axis=1)
        field, foot = run_steps(steps, total, reach, scalars, field, foot, u, v, mats)
    return field[:, total:total + width].transpose(0, 2, 1, 3), foot


def solution(mesh):
    return jax.shard_map(
        local,
        mesh=mesh,
        in_specs=(
            P("rcp", None, "lon", None),
            P("rcp", None, None, None, "lon", None),
            P("rcp", "lon", None, None),
            P(),
            P("rcp"),
            P("rcp"),
            P("rcp"),
        ),
        out_specs=(P("rcp", None, "lon", None), P("rcp", "lon", None)),
        check_vma=False,
    )
```

```python
import functools

import jax
import jax.numpy as jnp
from jax import lax
from jax.experimental import pallas as pl
from jax.experimental.pallas import tpu as pltpu
from jax.sharding import PartitionSpec as P

CHUNKS = ((0, 1, 2), (3, 4, 5))
PARTS = 4
SMEM = pl.BlockSpec(memory_space=pltpu.SMEM)
VMEM = pl.BlockSpec(memory_space=pltpu.VMEM)
LIMIT = pltpu.CompilerParams(vmem_limit_bytes=48 << 20)


def cost(nbytes):
    return pl.CostEstimate(flops=int(nbytes), bytes_accessed=int(nbytes), transcendentals=0)


def flip(block, bit):
    count = lax.axis_size("rcp")
    return lax.ppermute(block, "rcp", [(i, i ^ (1 << bit)) for i in range(count)])


def along(block, distance):
    count = lax.axis_size("lon")
    return lax.ppermute(block, "lon", [(i, (i + distance) % count) for i in range(count)])


def owned_pieces(flux, owners):
    count = lax.axis_size("rcp")
    block = flux.shape[2] // PARTS
    me = lax.axis_index("rcp")
    if count != PARTS:
        mine = (owners == me)[None, :, None, None, None]
        full = lax.psum(jnp.where(mine, flux, 0.0), "rcp")
        cuts = [full[:, :, m * block:(m + 1) * block] for m in range(PARTS)]
        return [c[0] for c in cuts], [c[1] for c in cuts], jnp.arange(PARTS, dtype=jnp.int32)

    def piece(comp, mask):
        return lax.dynamic_slice_in_dim(flux[comp], (me ^ mask) * block, block, axis=1)

    same_x = ((owners & 1) == (me & 1))[:, None, None, None]
    same_y = ((owners >> 1) == (me >> 1))[:, None, None, None]
    from_x = flip(jnp.stack([piece(0, 3), piece(0, 1)]), 0)
    from_y = flip(jnp.stack([piece(1, 3), piece(1, 2)]), 1)
    v_x = flip(jnp.where(same_y, piece(1, 1), from_y[0]), 0)
    u_y = flip(jnp.where(same_x, piece(0, 2), from_x[0]), 1)
    u_own = jnp.where(same_y, jnp.where(same_x, piece(0, 0), from_x[1]), u_y)
    v_own = jnp.where(same_x, jnp.where(same_y, piece(1, 0), from_y[1]), v_x)
    u2, v1 = flip(u_own, 1), flip(v_own, 0)
    u1, v2 = flip(u_own, 0), flip(v_own, 1)
    u3, v3 = flip(u2, 0), flip(v1, 1)
    part = jnp.stack([me ^ m for m in range(PARTS)]).astype(jnp.int32)
    return [u_own, u1, u2, u3], [v_own, v1, v2, v3], part


def edge_entries(steps, width):
    west, east = [], []
    for k in range(steps):
        reach = steps - 1 - k
        west += [(0, k, c) for c in range(reach + 1)] + [(1, k, c) for c in range(reach)]
        east += [(comp, k, width - reach + c) for comp in (0, 1) for c in range(reach)]
    return west, east


def edges_kernel(entries, part_ref, *refs):
    block = refs[0].shape[1]
    pieces, outs = (refs[:PARTS], refs[PARTS:2 * PARTS]), refs[2 * PARTS:]
    for out, wanted in zip(outs, entries):
        for i, (comp, k, c) in enumerate(wanted):
            for m in range(PARTS):
                rows = pl.ds(pl.multiple_of(part_ref[m] * block, block), block)
                out[i, rows, :] = pieces[comp][m][k, :, c, :]


def pick_edges(part, u, v):
    steps, block, width, lat = u[0].shape
    entries = edge_entries(steps, width)
    outs = pl.pallas_call(
        functools.partial(edges_kernel, [e for e in entries if e]),
        out_shape=[jax.ShapeDtypeStruct((len(e), PARTS * block, lat), jnp.float32) for e in entries if e],
        in_specs=[SMEM] + [VMEM] * (2 * PARTS),
        out_specs=[VMEM] * sum(bool(e) for e in entries),
        compiler_params=LIMIT,
        cost_estimate=cost(8 * u[0].size * 4),
        name="edges",
    )(part, *u, *v)
    return outs if len(outs) == 2 else (outs[0], None)


def assemble_kernel(part_ref, *refs):
    pieces, outs = (refs[:PARTS], refs[PARTS:2 * PARTS]), refs[2 * PARTS:]
    steps, block = refs[0].shape[:2]
    for k in range(steps):
        for comp in (0, 1):
            for m in range(PARTS):
                rows = pl.ds(pl.multiple_of(part_ref[m] * block, block), block)
                outs[comp][k, :, rows, :] = jnp.swapaxes(pieces[comp][m][k], 0, 1)


def assemble(part, u, v):
    steps, block, width, lat = u[0].shape
    return pl.pallas_call(
        assemble_kernel,
        out_shape=[jax.ShapeDtypeStruct((steps, width, PARTS * block, lat), jnp.float32)] * 2,
        in_specs=[SMEM] + [VMEM] * (2 * PARTS),
        out_specs=[VMEM] * 2,
        compiler_params=LIMIT,
        cost_estimate=cost(16 * u[0].size * 4),
        name="assemble",
    )(part, *u, *v)


def mats_kernel(owner_ref, packed_ref, out_ref):
    steps, lev = out_ref.shape[0], out_ref.shape[2]
    groups, lanes = packed_ref.shape[1], packed_ref.shape[3]
    lane = lax.broadcasted_iota(jnp.int32, (lev, lanes), 1)
    for s in range(steps):
        for g in range(groups):
            packed = packed_ref[owner_ref[s], g]
            high = packed.astype(jnp.bfloat16).astype(jnp.float32)
            low = packed - high
            for k in range(lanes // lev):
                def at(x, place):
                    return pltpu.roll(x, (place - k) * lev % lanes, 1) if place != k else x
                row = jnp.where(lane < lev, at(high, 0), jnp.where(lane < 2 * lev, at(high, 1), at(low, 2)))
                out_ref[s, g * (lanes // lev) + k] = row[:, :3 * lev].astype(jnp.bfloat16)


def prepare_mats(mixing, owner, lat):
    width, lev, _ = mixing.shape
    pack = lat // lev
    packed = mixing.reshape(width // pack, pack, lev, lev).transpose(0, 2, 1, 3)
    packed = packed.reshape(width // pack, lev, lat)
    packed = jnp.concatenate([along(packed[-1:], 1), packed, along(packed[:1], -1)], axis=0)
    count = lax.axis_size("rcp")
    slots = packed[None]
    if count == PARTS:
        me = lax.axis_index("rcp")
        for bit in range(2):
            slots = jnp.concatenate([slots, flip(slots, bit)], axis=0)
        owner = owner ^ me.astype(owner.dtype)
    else:
        slots = lax.all_gather(slots, "rcp", axis=0, tiled=True)
    return pl.pallas_call(
        mats_kernel,
        out_shape=jax.ShapeDtypeStruct((owner.shape[0], width + 2 * pack, lev, 3 * lev), jnp.bfloat16),
        in_specs=[SMEM, VMEM],
        out_specs=VMEM,
        compiler_params=LIMIT,
        cost_estimate=cost(owner.shape[0] * width * lev * lat * 2),
        name="mats",
    )(owner, slots)


def steps_kernel(first_step, steps, edges, has_left, last_chunk, rlon_ref, rlat_ref, rel_ref, start_ref,
                 field_ref, west_ref, east_ref, foot_ref, u_ref, v_ref, mats_ref, right_ref, *rest):
    left_ref = None
    if has_left:
        left_ref, rest = rest[0], rest[1:]
    if last_chunk:
        out_ref, foot_out_ref, a_ref, b_ref, ue_ref, ve_ref = rest
    else:
        out_ref, wout_ref, eout_ref, foot_out_ref, a_ref, b_ref, ue_ref, ve_ref = rest
    halo = steps
    count, ext, lev, lat = a_ref.shape
    width = ext - 2 * halo
    reach = halo - 1
    nlon = width * lax.axis_size("lon")
    mat_pad = (mats_ref.shape[1] - width) // 2 - halo
    lane = lax.broadcasted_iota(jnp.int32, (lev, lat), 1)
    lane_row = lax.broadcasted_iota(jnp.int32, (1, lat), 1)
    first = lane == 0
    last = lane == lat - 1

    for r in range(count):
        a_ref[r, :halo] = west_ref[r]
        a_ref[r, halo + width:] = east_ref[r]
        if field_ref.shape[1] == lev and first_step == 0:
            a_ref[r, halo:halo + width] = jnp.swapaxes(field_ref[r], 0, 1)
        else:
            a_ref[r, halo:halo + width] = field_ref[r]
    for i, (comp, k, c) in enumerate(edges[0]):
        (ue_ref, ve_ref)[comp][k, reach + width + c] = right_ref[i]
    for i, (comp, k, c) in enumerate(edges[1]):
        (ue_ref, ve_ref)[comp][k, reach + c - width] = left_ref[i]
    for k in range(steps):
        ue_ref[k, reach:reach + width] = u_ref[k]
        ve_ref[k, reach:reach + width] = v_ref[k]
    foot_out_ref[...] = foot_ref[...]

    for k in range(steps):
        step = first_step + k
        src, dst = ((a_ref, b_ref), (b_ref, a_ref))[k % 2]
        for r in range(count):
            col = lax.rem(rlon_ref[r] - start_ref[0] + halo + nlon, nlon)

            @pl.when((rel_ref[r] == step) & (col < ext))
            def _():
                row = src[r, pl.ds(col, 1), 0:1, :]
                src[r, pl.ds(col, 1), 0:1, :] = row + jnp.where(
                    lane_row == rlat_ref[r], 1.0, 0.0
                )[None]

        def column(c, carry, src=src, dst=dst, k=k):
            j = c - 1
            uw = ue_ref[k, j]
            un = ue_ref[k, j + 1]
            v = ve_ref[k, j]
            vs = jnp.where(first, 0.0, v)
            vn = jnp.where(last, 0.0, pltpu.roll(v, lat - 1, 1))
            cw = jnp.maximum(uw, 0.0)
            ce = -jnp.minimum(un, 0.0)
            cs = jnp.maximum(vs, 0.0)
            cn = -jnp.minimum(vn, 0.0)
            c0 = 1.0 + (jnp.minimum(uw, 0.0) - jnp.maximum(un, 0.0)) + (
                jnp.minimum(vs, 0.0) - jnp.maximum(vn, 0.0)
            )
            his, los = [], []
            for r in range(count):
                q = src[r, c]
                p = c0 * q + cw * src[r, c - 1] + ce * src[r, c + 1]
                p = p + cs * pltpu.roll(q, 1, 1) + cn * pltpu.roll(q, lat - 1, 1)
                hi = p.astype(jnp.bfloat16)
                his.append(hi)
                los.append((p - hi.astype(jnp.float32)).astype(jnp.bfloat16))
            hi = jnp.concatenate(his, axis=1)
            lo = jnp.concatenate(los, axis=1)
            new = jnp.dot(
                mats_ref[step, c + mat_pad],
                jnp.concatenate([hi, lo, hi], axis=0),
                preferred_element_type=jnp.float32,
            )
            for r in range(count):
                dst[r, c] = new[:, r * lat:(r + 1) * lat]
            return carry

        lax.fori_loop(k + 1, ext - k - 1, column, 0, unroll=2)
        for r in range(count):
            foot_out_ref[r] = foot_out_ref[r] + dst[r, halo:halo + width, 0, :]

    final = (a_ref, b_ref)[steps % 2]
    for r in range(count):
        if last_chunk:
            out_ref[r] = jnp.swapaxes(final[r, halo:halo + width], 0, 1)
        else:
            out_ref[r] = final[r, halo:halo + width]
            wout_ref[r] = final[r, halo:halo + wout_ref.shape[1]]
            eout_ref[r] = final[r, halo + width - eout_ref.shape[1]:halo + width]


def run_steps(rows, next_halo, last_chunk, scalars, field, west, east, foot, u, v, mats, right, left):
    count, width, lat = foot.shape
    steps, lev = u.shape[0], u.shape[2]
    ext = width + 2 * steps
    tiles = jax.ShapeDtypeStruct
    if last_chunk:
        outs = [tiles((count, lev, width, lat), jnp.float32)]
    else:
        outs = [tiles((count, width, lev, lat), jnp.float32)]
        outs += [tiles((count, next_halo, lev, lat), jnp.float32)] * 2
    outs.append(tiles(foot.shape, jnp.float32))
    extra = [right] + ([left] if left is not None else [])
    return pl.pallas_call(
        functools.partial(
            steps_kernel, rows[0], steps, edge_entries(steps, width), left is not None, last_chunk
        ),
        out_shape=outs,
        in_specs=[SMEM] * 4 + [VMEM] * (7 + len(extra)),
        out_specs=[VMEM] * len(outs),
        scratch_shapes=[
            pltpu.VMEM((count, ext, lev, lat), jnp.float32),
            pltpu.VMEM((count, ext, lev, lat), jnp.float32),
            pltpu.VMEM((steps, width + 2 * steps - 1, lev, lat), jnp.float32),
            pltpu.VMEM((steps, width + 2 * steps - 2, lev, lat), jnp.float32),
        ],
        compiler_params=LIMIT,
        cost_estimate=pl.CostEstimate(
            flops=int(steps * count * width * lev * lev * lat * 6),
            bytes_accessed=int(8 * count * width * lev * lat), transcendentals=0,
        ),
        name="steps_%d" % rows[0],
    )(*scalars, field, west, east, foot, u, v, mats, *extra)


def local(adj_in, mass_flux, mixing, window_owner, receptor_lon, receptor_lat, release_step):
    count, lev, width, lat = adj_in.shape
    start = (lax.axis_index("lon") * width).astype(jnp.int32)[None]
    scalars = (receptor_lon, receptor_lat, release_step, start)
    field = adj_in
    halo = len(CHUNKS[0])
    east_edge = adj_in[:, :, width - halo:].transpose(0, 2, 1, 3)
    west_edge = adj_in[:, :, :halo].transpose(0, 2, 1, 3)
    mats = prepare_mats(mixing[0], window_owner, lat)
    foot = jnp.zeros((count, width, lat), jnp.float32)
    for n, rows in enumerate(CHUNKS):
        west, east = along(east_edge, 1), along(west_edge, -1)
        u, v, part = owned_pieces(mass_flux[0, :, rows[0]:rows[-1] + 1], window_owner[rows[0]:rows[-1] + 1])
        to_west, to_east = pick_edges(part, u, v)
        right = along(to_west, -1)
        left = along(to_east, 1) if to_east is not None else None
        u, v = assemble(part, u, v)
        last = n + 1 == len(CHUNKS)
        out = run_steps(rows, 0 if last else len(CHUNKS[n + 1]), last, scalars, field, west, east, foot,
                        u, v, mats, right, left)
        if last:
            return tuple(out)
        field, west_edge, east_edge, foot = out


def solution(mesh):
    return jax.shard_map(
        local,
        mesh=mesh,
        in_specs=(
            P("rcp", None, "lon", None),
            P("rcp", None, None, None, "lon", None),
            P("rcp", "lon", None, None),
            P(),
            P("rcp"),
            P("rcp"),
            P("rcp"),
        ),
        out_specs=(P("rcp", None, "lon", None), P("rcp", "lon", None)),
        check_vma=False,
    )
```
